512 devices in a mesh: gx: 16 (over y, z_lo), gy: 32 (over z_hi, x, core).
Axes of the slice: x: 4, y: 4, z: 16 (z_hi: 4, z_lo: 4; z = z_hi * 4 + z_lo), core: 2. Of those that a mesh axis runs over, the one named last changes fastest.
Arguments:
- right_side: float32 [16, 64, 32768], P('gx', None, 'gy')
- weights: float32 [16, 32768], P('gx', 'gy'), may hold values from 0.25 to 1.75
- signs: int32 [16, 32768], P('gx', 'gy'), may hold values from 0 to 1
- face_map: int32 [16, 32768], P('gx', 'gy'), may hold values from 0 to 1023, as said below
- pattern: int32 [16, 8, 256], P('gx', None, 'gy'), may hold values 0 or 1
- factor: float32 [16, 1024, 32768], P('gx', None, 'gy')
Outputs:
- solution_field: float32 [16, 64, 32768], P('gx', None, 'gy')
- residual: float32 [16, 64, 32768], P('gx', None, 'gy')
The draws below stay inside these ranges and needn't reach their ends.
Inputs may be any that keep to these rules, and one draw needn't show every extreme that they name: `face_map`: each subdomain's block of 1024 entries is a permutation of 0 to 1023.
All inputs are finite; a program needn't handle non-finite values. No bound on the sum of `pattern` on one device may be relied on, other than what follows from the above.
Results may differ from the reference program's by a relative error of at most 0.0003.
Values sent between devices are 32-bit elements; how exact they have to be, the bound alone decides.
A program may use at most 64 MiB of HBM per device.

```python
import jax
import jax.numpy as jnp
from jax import lax

L = 1024
CASES = 64
BLK = 128
ITERS = 4
NB = 8
FACE = 256
SUB_X = 16
SUB_Y = 32


def draw_right_side(key, part):
    rank = (jnp.arange(SUB_X)[:, None] * SUB_Y + jnp.arange(SUB_Y)[None, :]).astype(jnp.float32)
    device_ramp = 3.0 ** (rank / (SUB_X * SUB_Y - 1))
    base_draw = jax.random.normal(jax.random.fold_in(key, 1), (SUB_X, CASES, SUB_Y, L), jnp.float32)
    result = base_draw * device_ramp[:, None, :, None]
    return result.reshape(SUB_X, CASES, SUB_Y * L)


def draw_face_map(key, part):
    key_list = jax.random.split(jax.random.fold_in(key, 7), SUB_X * SUB_Y)
    perms = jax.vmap(lambda one_key: jax.random.permutation(one_key, L))(key_list)
    return perms.reshape(SUB_X, SUB_Y * L).astype(jnp.int32)


def draw_factor(key, part):
    spread = 0.5
    off_part = jax.random.normal(jax.random.fold_in(key, 3), (SUB_X, L, SUB_Y, L), jnp.float32) * (spread / L ** 0.5)
    diag_vals = 1.0 + jax.random.uniform(jax.random.fold_in(key, 4), (SUB_X, L, SUB_Y, 1), jnp.float32)
    identity = jnp.eye(L, dtype=jnp.float32)[None, :, None, :]
    return (off_part + identity * diag_vals).reshape(SUB_X, L, SUB_Y * L)


def place_ends(array, own_key, low, high):
    longest = array.shape.index(max(array.shape))
    spots = []
    for shift in (0, 1):
        where = [jax.random.randint(jax.random.fold_in(own_key, axis), (), 0, length) for axis, length in enumerate(array.shape)]
        where[longest] = (where[longest] + shift) % array.shape[longest]
        spots.append(tuple(where))
    return array.at[spots[0]].set(low).at[spots[1]].set(high)


def setup_inputs(seed: int = 0) -> dict:
    key_of = jax.random.split(jax.random.key(seed), 7)
    return {
        "right_side": draw_right_side(jax.random.fold_in(key_of[6], 71), 0),
        "weights": jnp.clip(1.0 + 0.15 * jax.random.normal(key_of[1], (SUB_X, SUB_Y * L), jnp.float32), 0.25, 1.75),
        "signs": place_ends(jax.random.randint(key_of[2], (SUB_X, SUB_Y * L), 0, 2), jax.random.fold_in(key_of[2], 1), 0, 1).astype(jnp.int32),
        "face_map": draw_face_map(jax.random.fold_in(key_of[6], 71), 0),
        "pattern": place_ends((jax.random.randint(key_of[4], (SUB_X, NB, SUB_Y * NB), 0, 2) < 1).astype(jnp.int32), jax.random.fold_in(key_of[4], 1), 0, 1),
        "factor": draw_factor(jax.random.fold_in(key_of[6], 71), 0),
    }


HIGH = lax.Precision.HIGHEST

def partner(field, face_order, inverse):
    face_vals = jnp.take_along_axis(field, jnp.broadcast_to(face_order, field.shape), axis=3)
    north_vals = face_vals[..., 0:FACE]
    south_vals = face_vals[..., FACE:2 * FACE]
    west_vals = face_vals[..., 2 * FACE:3 * FACE]
    east_vals = face_vals[..., 3 * FACE:]
    empty_row = jnp.zeros_like(north_vals[:1])
    from_north = jnp.concatenate([empty_row, south_vals[:-1]], axis=0)
    from_south = jnp.concatenate([north_vals[1:], empty_row], axis=0)
    empty_col = jnp.zeros_like(north_vals[:, :, :1])
    from_west = jnp.concatenate([empty_col, east_vals[:, :, :-1]], axis=2)
    from_east = jnp.concatenate([west_vals[:, :, 1:], empty_col], axis=2)
    stacked = jnp.concatenate([from_north, from_south, from_west, from_east], axis=3)
    return jnp.take_along_axis(stacked, jnp.broadcast_to(inverse, field.shape), axis=3)

def inner_prod(left, right):
    return jnp.einsum('xayl,xbyl->ab', left, right, precision=HIGH)

def reference(right_side, weights, signs, face_map, pattern, factor):
    loads = right_side.reshape(SUB_X, CASES, SUB_Y, L)
    weighting = weights.reshape(SUB_X, 1, SUB_Y, L)
    jump_sign = (2 * signs - 1).astype(jnp.float32).reshape(SUB_X, 1, SUB_Y, L)
    face_order = face_map.reshape(SUB_X, 1, SUB_Y, L).astype(jnp.int32)
    inverse = jnp.argsort(face_order, axis=-1).astype(jnp.int32)
    keep_blocks = jnp.maximum(pattern.reshape(SUB_X, NB, SUB_Y, NB), jnp.eye(NB, dtype=jnp.int32)[None, :, None, :])
    keep_full = jnp.repeat(jnp.repeat(keep_blocks.astype(jnp.float32), BLK, axis=1), BLK, axis=3)
    factor_masked = factor.reshape(SUB_X, L, SUB_Y, L) * keep_full

    def operate(field):
        lifted = field + 0.5 * jump_sign * partner(field, face_order, inverse)
        halfway = jnp.einsum('xcyi,xiyj->xcyj', lifted, factor_masked, precision=HIGH)
        local_out = jnp.einsum('xcyj,xiyj->xcyi', halfway, factor_masked, precision=HIGH)
        return local_out + 0.5 * partner(jump_sign * local_out, face_order, inverse)

    def apply_left(matrix, field):
        return jnp.einsum('ab,xayl->xbyl', matrix, field, precision=HIGH)
    solution = jnp.zeros_like(loads)
    resid = loads
    direction = weighting * resid
    for iteration in range(ITERS):
        images = operate(direction)
        gram_matrix = inner_prod(direction, images)
        lower_factor = jnp.linalg.cholesky(gram_matrix)
        step_size = jax.scipy.linalg.cho_solve((lower_factor, True), inner_prod(direction, resid))
        solution = solution + apply_left(step_size, direction)
        resid = resid - apply_left(step_size, images)
        if iteration + 1 < ITERS:
            precond = weighting * resid
            update = -jax.scipy.linalg.cho_solve((lower_factor, True), inner_prod(images, precond))
            direction = precond + apply_left(update, direction)
    return (solution.reshape(SUB_X, CASES, SUB_Y * L), resid.reshape(SUB_X, CASES, SUB_Y * L))
```

```python
import functools

import jax
import jax.numpy as jnp
from jax import lax
from jax.experimental import pallas as pl
from jax.experimental.pallas import tpu as pltpu
from jax.sharding import PartitionSpec as P

ITERS = 4
MESH = pl.DeviceIdType.MESH
HIGH = lax.Precision.HIGHEST
F32 = jnp.float32
BF16 = jnp.bfloat16
NN = (((1,), (0,)), ((), ()))
NT = (((1,), (1,)), ((), ()))
TN = (((0,), (0,)), ((), ()))
Z_PARTS = 4


def split2(value):
    high = value.astype(BF16)
    low = (value - high.astype(F32)).astype(BF16)
    return high, low


def split3(value):
    high = value.astype(BF16)
    rest = value - high.astype(F32)
    middle = rest.astype(BF16)
    low = (rest - middle.astype(F32)).astype(BF16)
    return high, middle, low


def dot(left, right, dims=NN):
    return lax.dot_general(left, right, dims, preferred_element_type=F32)


def invert_small(entries):
    count = len(entries)
    rows = [list(row) + [None] * count for row in entries]
    work = [[entries[r][c] for c in range(count)] for r in range(count)]
    inverse = [[None] * count for _ in range(count)]
    for pivot in range(count):
        scale = 1.0 / work[pivot][pivot]
        for c in range(count):
            if c > pivot:
                work[pivot][c] = work[pivot][c] * scale
            if c < pivot:
                inverse[pivot][c] = inverse[pivot][c] * scale
        inverse[pivot][pivot] = scale
        for r in range(count):
            if r == pivot:
                continue
            factor = work[r][pivot]
            for c in range(count):
                if c > pivot:
                    work[r][c] = work[r][c] - factor * work[pivot][c]
                if c < pivot:
                    inverse[r][c] = inverse[r][c] - factor * inverse[pivot][c]
            inverse[r][pivot] = -factor * scale
    return inverse


def eliminate(tiles, size, block):
    wide = len(tiles[0])
    sublane = lax.broadcasted_iota(jnp.int32, (8, 128), 0)
    for start in range(0, size, block):
        home, first = start // 8, start % 8
        columns = [
            [jnp.broadcast_to(tile[0][:, start + r : start + r + 1], (8, 128)) for tile in tiles]
            for r in range(block)
        ]
        rows = [
            [jnp.broadcast_to(tiles[home][h][first + r : first + r + 1, :], (8, 128)) for h in range(wide)]
            for r in range(block)
        ]
        entries = [
            [jnp.broadcast_to(columns[c][home][first + r : first + r + 1, :], (8, 128)) for c in range(block)]
            for r in range(block)
        ]
        inverse = invert_small(entries)
        scaled = [
            [sum(inverse[r][c] * rows[c][h] for c in range(block)) for h in range(wide)]
            for r in range(block)
        ]
        for t in range(len(tiles)):
            for h in range(wide):
                updated = tiles[t][h]
                for r in range(block):
                    updated = updated - columns[r][t] * scaled[r][h]
                if t == home:
                    for r in range(block):
                        updated = jnp.where(sublane == first + r, scaled[r][h], updated)
                tiles[t][h] = updated
    return tiles


def kernel(
    cfg,
    loads_ref, weights_ref, signs_ref, map_ref, pattern_ref, factor_hbm,
    sol_ref, res_ref,
    stage_ref, zh_ref, zl_ref, perm_ref, dir_ref, img_ref, imgp_ref, lin_ref, linp_ref, s_ref, sp_ref,
    half_ref, y_ref, wp_ref, sg_ref, sgp_ref, first_out, first_in, halo_out, halo_in,
    gram_ref, scat_ref, part_ref, line_ref, gath_ref,
    load_sem, first_send, first_recv, halo_send, halo_recv,
    scat_send, scat_recv, line_send, line_recv, gath_send, gath_recv,
):
    rows_y, z_lo, z_hi, cols_j, chunk = cfg
    plane, depth = rows_y * cols_j, z_lo * z_hi
    gx, gy = lax.axis_index("gx"), lax.axis_index("gy")
    size_x, size_y = rows_y * z_lo, z_hi * cols_j
    my_y, my_lo = gx // z_lo, gx % z_lo
    my_hi, my_j = gy // cols_j, gy % cols_j
    my_plane = my_y * cols_j + my_j
    my_depth = my_hi * z_lo + my_lo
    cases, unknowns = loads_ref.shape[1], loads_ref.shape[2]
    face = unknowns // 4
    north = ((gx + size_x - 1) % size_x, gy)
    south = ((gx + 1) % size_x, gy)
    west = (gx, (gy + size_y - 1) % size_y)
    east = (gx, (gy + 1) % size_y)
    ways = (north, south, west, east)
    opposite = (1, 0, 3, 2)

    def plane_peer(step):
        peer = (my_plane + step) % plane
        return peer, ((peer // cols_j) * z_lo + my_lo, my_hi * cols_j + peer % cols_j)

    def line_peer(step):
        peer = (my_depth + step) % depth
        return peer, (my_y * z_lo + peer % z_lo, (peer // z_lo) * cols_j + my_j)

    load = pltpu.make_async_copy(factor_hbm.at[0], stage_ref, load_sem)
    load.start()

    barrier = pltpu.get_barrier_semaphore()

    def signal(device):
        pl.semaphore_signal(barrier, inc=1, device_id=device, device_id_type=MESH)

    def greet_plane(step, carry):
        signal(plane_peer(step)[1])
        return carry

    def greet_line(step, carry):
        signal(line_peer(step)[1])
        return carry

    lax.fori_loop(1, plane, greet_plane, 0)
    lax.fori_loop(1, depth, greet_line, 0)
    for way in ways:
        signal(way)

    def build_perm(step, carry):
        start = pl.multiple_of(step * 128, 128)
        index = lax.broadcasted_iota(jnp.int32, (128, unknowns), 0) + step * 128
        perm_ref[pl.ds(start, 128), :] = jnp.where(index == map_ref[...], 1.0, 0.0).astype(BF16)
        return carry

    lax.fori_loop(0, unknowns // 128, build_perm, 0)
    weighting = weights_ref[...]
    sigma = (2 * signs_ref[...] - 1).astype(F32)

    def to_faces(value, out_ref, rows):
        parts = jnp.concatenate(split3(value), axis=0)
        for f in range(4):
            moved = dot(parts, perm_ref[:, f * face : (f + 1) * face])
            out_ref[f] = moved[:rows] + moved[rows : 2 * rows] + moved[2 * rows :]

    def from_faces(in_ref, rows):
        has = (gx > 0, gx < size_x - 1, gy > 0, gy < size_y - 1)
        blocks = [jnp.where(has[f], in_ref[f], 0.0) for f in range(4)]
        parts = jnp.concatenate(split3(jnp.concatenate(blocks, axis=1)), axis=0)
        moved = dot(parts, perm_ref[...], NT)
        return moved[:rows] + moved[rows : 2 * rows] + moved[2 * rows :]

    def exchange(out_ref, in_ref, send_sem, recv_sem):
        copies = []
        for f in range(4):
            copies.append(
                pltpu.make_async_remote_copy(
                    src_ref=out_ref.at[f],
                    dst_ref=in_ref.at[opposite[f]],
                    send_sem=send_sem.at[f],
                    recv_sem=recv_sem.at[opposite[f]],
                    device_id=ways[f],
                    device_id_type=MESH,
                )
            )
        return copies

    first = loads_ref[0] * weighting
    dir_ref[...] = first
    extra = jnp.concatenate([weighting, sigma, jnp.zeros((6, unknowns), F32)], axis=0)
    to_faces(jnp.concatenate([first, extra], axis=0), first_out, cases + 8)
    pl.semaphore_wait(barrier, (plane - 1) + (depth - 1) + 4)
    copies = exchange(first_out, first_in, first_send, first_recv)
    for copy in copies:
        copy.start()

    load.wait()
    blocks = pattern_ref.shape[1]
    block_size = unknowns // blocks

    def mask_rows(i, carry):
        start = pl.multiple_of(i * block_size, block_size)
        for j in range(blocks):
            keep = jnp.where(i == j, 1, pattern_ref[0, i, j]).astype(F32)
            value = stage_ref[pl.ds(start, block_size), j * block_size : (j + 1) * block_size] * keep
            high, low = split2(value)
            zh_ref[pl.ds(start, block_size), j * block_size : (j + 1) * block_size] = high
            zl_ref[pl.ds(start, block_size), j * block_size : (j + 1) * block_size] = low
        return carry

    lax.fori_loop(0, blocks, mask_rows, 0)

    def local_product(lifted):
        high, low = split2(lifted)
        both = jnp.concatenate([high, low], axis=0)
        for n in range(4):
            tile = slice(n * face, (n + 1) * face)
            wide = dot(both, zh_ref[:, tile])
            half_ref[:, tile] = wide[:cases] + wide[cases:] + dot(high, zl_ref[:, tile])
        high, low = split2(half_ref[...])
        both = jnp.concatenate([high, low], axis=0)
        for n in range(4):
            tile = slice(n * face, (n + 1) * face)
            wide = dot(both, zh_ref[tile, :], NT)
            y_ref[:, tile] = wide[:cases] + wide[cases:] + dot(high, zl_ref[tile, :], NT)

    for copy in copies:
        copy.wait()
    moved = from_faces(first_in, cases + 8)
    wp_ref[...] = moved[cases : cases + 1]
    sgp_ref[...] = moved[cases + 1 : cases + 2]
    sg_ref[...] = sigma * sgp_ref[...] * sgp_ref[...]

    def apply(slot, lifted, out_ref, outp_ref):
        local_product(lifted)
        to_faces(y_ref[...], halo_out.at[slot], cases)
        copies = exchange(halo_out.at[slot], halo_in.at[slot], halo_send.at[slot], halo_recv.at[slot])
        for copy in copies:
            copy.start()
        return copies

    def finish(slot, copies, out_ref, outp_ref):
        for copy in copies:
            copy.wait()
        other = from_faces(halo_in.at[slot], cases)
        out_ref[...] = y_ref[...] + 0.5 * (sgp_ref[...] * other)
        outp_ref[...] = other + 0.5 * (sg_ref[...] * y_ref[...])

    finish(0, apply(0, first + 0.5 * (sigma * moved[:cases]), img_ref, imgp_ref), img_ref, imgp_ref)
    lin_ref[...] = img_ref[...]
    linp_ref[...] = imgp_ref[...]
    res_ref[0] = loads_ref[0]
    sol_ref[0] = jnp.zeros((cases, unknowns), F32)

    def send_all(count, peer_of, source_of, dst_ref, send_sem, recv_sem):
        def body(step, carry):
            peer, device = peer_of(step)
            pltpu.make_async_remote_copy(
                src_ref=source_of(peer),
                dst_ref=dst_ref,
                send_sem=send_sem,
                recv_sem=recv_sem,
                device_id=device,
                device_id_type=MESH,
            ).start()
            return carry

        lax.fori_loop(1, count, body, 0)

    def wait_bytes(ref, count, sem):
        pltpu.make_async_copy(ref.at[pl.ds(0, count)], ref.at[pl.ds(0, count)], sem).wait()

    def iteration(k, carry):
        last = k == ITERS - 1
        weighted_res = weighting * res_ref[0]
        weighted_img = weighting * img_ref[...]
        left = lax.dot_general(
            dir_ref[...], jnp.concatenate([img_ref[...], res_ref[0]], axis=0), NT,
            precision=HIGH, preferred_element_type=F32,
        )
        right = lax.dot_general(
            img_ref[...], jnp.concatenate([weighted_res, weighted_img], axis=0), NT,
            precision=HIGH, preferred_element_type=F32,
        )
        per_half = cases // chunk
        for t in range(per_half):
            gram_ref[k, t] = left[t * chunk : (t + 1) * chunk]
            gram_ref[k, per_half + t] = right[t * chunk : (t + 1) * chunk]
        send_all(plane, plane_peer, lambda peer: gram_ref.at[k, peer], scat_ref.at[k, my_plane],
                 scat_send.at[k], scat_recv.at[k])
        scat_ref[k, my_plane] = gram_ref[k, my_plane]

        @pl.when(k < ITERS - 1)
        def _():
            apply(k + 1, weighted_img + 0.5 * (sg_ref[...] * (wp_ref[...] * imgp_ref[...])), s_ref, sp_ref)

        wait_bytes(scat_ref.at[k], plane - 1, scat_recv.at[k])
        part = scat_ref[k, 0]
        for p in range(1, plane):
            part = part + scat_ref[k, p]
        part_ref[k, 0] = part
        line_ref[k, my_depth] = part
        send_all(depth, line_peer, lambda peer: part_ref.at[k, 0], line_ref.at[k, my_depth],
                 line_send.at[k], line_recv.at[k])
        wait_bytes(line_ref.at[k], depth - 1, line_recv.at[k])
        total = line_ref[k, 0]
        for p in range(1, depth):
            total = total + line_ref[k, p]
        part_ref[k, 1] = total
        gath_ref[k, my_plane] = total
        send_all(plane, plane_peer, lambda peer: part_ref.at[k, 1], gath_ref.at[k, my_plane],
                 gath_send.at[k], gath_recv.at[k])

        @pl.when(k < ITERS - 1)
        def _():
            copies = exchange(halo_out.at[k + 1], halo_in.at[k + 1], halo_send.at[k + 1], halo_recv.at[k + 1])
            finish(k + 1, copies, s_ref, sp_ref)

        wait_bytes(gath_ref.at[k], plane - 1, gath_recv.at[k])
        tiles = []
        for t in range(cases // 8):
            tiles.append([])
            for h in range(2):
                at = h * cases + t * 8
                pieces = [
                    gath_ref[k, row // chunk, row % chunk : row % chunk + min(chunk, 8)]
                    for row in range(at, at + 8, min(chunk, 8))
                ]
                tiles[t].append(jnp.concatenate(pieces, axis=0))
        tiles = eliminate(tiles, cases, 4)
        solved_left = jnp.concatenate([tile[0] for tile in tiles], axis=0)
        solved_right = jnp.concatenate([tile[1] for tile in tiles], axis=0)
        step_size = solved_left[:, cases:]
        update = lax.dot_general(solved_right[:, cases:], step_size, NN, precision=HIGH,
                                 preferred_element_type=F32) - solved_right[:, :cases]

        def across(matrix, field):
            return lax.dot_general(matrix, field, TN, precision=HIGH, preferred_element_type=F32)

        sol_ref[0] = sol_ref[0] + across(step_size, dir_ref[...])
        res_ref[0] = res_ref[0] - across(step_size, img_ref[...])

        @pl.when(k < ITERS - 1)
        def _():
            lin_ref[...] = lin_ref[...] - across(step_size, s_ref[...])
            linp_ref[...] = linp_ref[...] - across(step_size, sp_ref[...])
            dir_ref[...] = weighting * res_ref[0] + across(update, dir_ref[...])
            img_ref[...] = lin_ref[...] + across(update, img_ref[...])
            imgp_ref[...] = linp_ref[...] + across(update, imgp_ref[...])

        wait_bytes(scat_ref.at[k], plane - 1, scat_send.at[k])
        wait_bytes(line_ref.at[k], depth - 1, line_send.at[k])
        wait_bytes(gath_ref.at[k], plane - 1, gath_send.at[k])
        return carry

    lax.fori_loop(0, ITERS, iteration, 0)


def local(cfg, right_side, weights, signs, face_map, pattern, factor):
    cases, unknowns = right_side.shape[1:]
    face = unknowns // 4
    rows_y, z_lo, z_hi, cols_j, chunk = cfg
    plane, depth = rows_y * cols_j, z_lo * z_hi
    field = pltpu.VMEM((cases, unknowns), F32)
    row = pltpu.VMEM((1, unknowns), F32)
    square = pltpu.VMEM((unknowns, unknowns), BF16)
    dma = pltpu.SemaphoreType.DMA
    return pl.pallas_call(
        functools.partial(kernel, cfg),
        out_shape=(jax.ShapeDtypeStruct(right_side.shape, F32),) * 2,
        in_specs=[pl.BlockSpec(memory_space=pltpu.VMEM)] * 4
        + [pl.BlockSpec(memory_space=pltpu.SMEM), pl.BlockSpec(memory_space=pl.ANY)],
        out_specs=(pl.BlockSpec(memory_space=pltpu.VMEM),) * 2,
        scratch_shapes=[
            pltpu.VMEM((unknowns, unknowns), F32), square, square, square,
            field, field, field, field, field, field, field,
            field, field, row, row, row,
            pltpu.VMEM((4, cases + 8, face), F32), pltpu.VMEM((4, cases + 8, face), F32),
            pltpu.VMEM((ITERS, 4, cases, face), F32), pltpu.VMEM((ITERS, 4, cases, face), F32),
            pltpu.VMEM((ITERS, plane, chunk, 128), F32), pltpu.VMEM((ITERS, plane, chunk, 128), F32),
            pltpu.VMEM((ITERS, 2, chunk, 128), F32), pltpu.VMEM((ITERS, depth, chunk, 128), F32),
            pltpu.VMEM((ITERS, plane, chunk, 128), F32),
            dma, dma((4,)), dma((4,)), dma((ITERS, 4)), dma((ITERS, 4)),
            dma((ITERS,)), dma((ITERS,)), dma((ITERS,)), dma((ITERS,)), dma((ITERS,)), dma((ITERS,)),
        ],
        compiler_params=pltpu.CompilerParams(
            collective_id=0, has_side_effects=True, vmem_limit_bytes=60 * 1024 * 1024
        ),
    )(right_side, weights, signs, face_map, pattern, factor)


def solution(mesh):
    size_x, size_y = mesh.shape["gx"], mesh.shape["gy"]
    z_lo = min(Z_PARTS, size_x // 2)
    z_hi = min(Z_PARTS, size_y // 2)
    rows_y, cols_j = size_x // z_lo, size_y // z_hi
    chunk = 128 // (rows_y * cols_j)
    return jax.shard_map(
        functools.partial(local, (rows_y, z_lo, z_hi, cols_j, chunk)),
        mesh=mesh,
        in_specs=(
            P("gx", None, "gy"),
            P("gx", "gy"),
            P("gx", "gy"),
            P("gx", "gy"),
            P("gx", None, "gy"),
            P("gx", None, "gy"),
        ),
        out_specs=(P("gx", None, "gy"), P("gx", None, "gy")),
        check_vma=False,
    )
```

```python
import functools

import jax
import jax.numpy as jnp
from jax import lax
from jax.experimental import pallas as pl
from jax.experimental.pallas import tpu as pltpu
from jax.sharding import PartitionSpec as P

ITERS = 4
MESH = pl.DeviceIdType.MESH
HIGH = lax.Precision.HIGHEST
F32 = jnp.float32
BF16 = jnp.bfloat16
NN = (((1,), (0,)), ((), ()))
NT = (((1,), (1,)), ((), ()))
TN = (((0,), (0,)), ((), ()))
Z_PARTS = 4


def split2(value):
    high = value.astype(BF16)
    low = (value - high.astype(F32)).astype(BF16)
    return high, low


def split3(value):
    high = value.astype(BF16)
    rest = value - high.astype(F32)
    middle = rest.astype(BF16)
    low = (rest - middle.astype(F32)).astype(BF16)
    return high, middle, low


def dot(left, right, dims=NN):
    return lax.dot_general(left, right, dims, preferred_element_type=F32)


def invert_small(entries):
    count = len(entries)
    rows = [list(row) + [None] * count for row in entries]
    work = [[entries[r][c] for c in range(count)] for r in range(count)]
    inverse = [[None] * count for _ in range(count)]
    for pivot in range(count):
        scale = 1.0 / work[pivot][pivot]
        for c in range(count):
            if c > pivot:
                work[pivot][c] = work[pivot][c] * scale
            if c < pivot:
                inverse[pivot][c] = inverse[pivot][c] * scale
        inverse[pivot][pivot] = scale
        for r in range(count):
            if r == pivot:
                continue
            factor = work[r][pivot]
            for c in range(count):
                if c > pivot:
                    work[r][c] = work[r][c] - factor * work[pivot][c]
                if c < pivot:
                    inverse[r][c] = inverse[r][c] - factor * inverse[pivot][c]
            inverse[r][pivot] = -factor * scale
    return inverse


def total(terms):
    while len(terms) > 1:
        terms = [terms[i] + terms[i + 1] if i + 1 < len(terms) else terms[i] for i in range(0, len(terms), 2)]
    return terms[0]


def eliminate(tiles, size, block):
    wide = len(tiles[0])
    sublane = lax.broadcasted_iota(jnp.int32, (8, 128), 0)

    def lane(tile, at):
        return jnp.broadcast_to(tile[:, at : at + 1], (8, 128))

    def row(tile, at):
        return jnp.broadcast_to(tile[at : at + 1, :], (8, 128))

    columns = [[lane(tile[0], r) for tile in tiles] for r in range(block)]
    for start in range(0, size, block):
        home, first = start // 8, start % 8
        span = range(block)
        ahead = start + block < size
        before = [[lane(tile[0], start + block + r) for tile in tiles] for r in span] if ahead else []
        inverse = invert_small([[row(columns[c][home], first + r) for c in span] for r in span])

        def eliminated(values, lines):
            scaled = [total([inverse[r][c] * lines[c] for c in span]) for r in span]
            out = []
            for t, value in enumerate(values):
                new = value - total([columns[r][t] * scaled[r] for r in span])
                if t == home:
                    for r in span:
                        new = jnp.where(sublane == first + r, scaled[r], new)
                out.append(new)
            return out

        following = [eliminated(b, [row(b[home], first + c) for c in span]) for b in before]
        for h in range(wide):
            done = eliminated([tile[h] for tile in tiles], [row(tiles[home][h], first + c) for c in span])
            for t, value in enumerate(done):
                tiles[t][h] = value
        columns = following
    return tiles


def ring(offset, count):
    return min(offset, count - offset)


def kernel(
    cfg,
    loads_ref, weights_ref, signs_ref, map_ref, pattern_ref, factor_hbm,
    sol_ref, res_ref,
    stage_ref, zh_ref, zl_ref, perm_ref, dir_ref, img_ref, imgp_ref, lin_ref, linp_ref, s_ref, sp_ref,
    dst_ref, ist_ref, sst_ref, cst_ref, half_ref, y_ref, wp_ref, sg_ref, sgp_ref, first_out, first_in, halo_out, halo_in,
    gram_ref, scat_ref, part_ref, line_ref, gath_ref,
    load_sem, first_send, first_recv, halo_send, halo_recv,
    scat_send, scat_recv, line_send, line_recv, gath_send, gath_recv,
):
    rows_y, z_lo, z_hi, cols_j, chunk = cfg
    plane, depth = rows_y * cols_j, z_lo * z_hi
    gx, gy = lax.axis_index("gx"), lax.axis_index("gy")
    size_x, size_y = rows_y * z_lo, z_hi * cols_j
    my_y, my_lo = gx // z_lo, gx % z_lo
    my_hi, my_j = gy // cols_j, gy % cols_j
    my_plane = my_y * cols_j + my_j
    my_depth = my_hi * z_lo + my_lo
    cases, unknowns = loads_ref.shape[1], loads_ref.shape[2]
    face = unknowns // 4
    north = ((gx + size_x - 1) % size_x, gy)
    south = ((gx + 1) % size_x, gy)
    west = (gx, (gy + size_y - 1) % size_y)
    east = (gx, (gy + 1) % size_y)
    ways = (north, south, west, east)
    opposite = (1, 0, 3, 2)

    def plane_peer(offset):
        peer_y = (my_y + offset[0]) % rows_y
        peer_j = ((my_j // 2 + offset[1]) % (cols_j // 2)) * 2 + (my_j + offset[2]) % 2
        return peer_y * cols_j + peer_j, (peer_y * z_lo + my_lo, my_hi * cols_j + peer_j)

    def line_peer(offset):
        peer = (my_depth + offset) % depth
        return peer, (my_y * z_lo + peer % z_lo, (peer // z_lo) * cols_j + my_j)

    plane_offsets = sorted(
        [(a, b, c) for a in range(rows_y) for b in range(cols_j // 2) for c in range(2) if a or b or c],
        key=lambda o: -(ring(o[0], rows_y) + ring(o[1], cols_j // 2) + 0.5 * o[2]),
    )
    line_offsets = sorted(range(1, depth), key=lambda o: -ring(o, depth))

    load = pltpu.make_async_copy(factor_hbm.at[0], stage_ref, load_sem)
    load.start()

    barrier = pltpu.get_barrier_semaphore()

    def signal(device):
        pl.semaphore_signal(barrier, inc=1, device_id=device, device_id_type=MESH)

    for offset in line_offsets:
        signal(line_peer(offset)[1])
    for way in ways:
        signal(way)
    for offset in plane_offsets:
        signal(plane_peer(offset)[1])

    def build_perm(step, carry):
        start = pl.multiple_of(step * 128, 128)
        index = lax.broadcasted_iota(jnp.int32, (128, unknowns), 0) + step * 128
        perm_ref[pl.ds(start, 128), :] = jnp.where(index == map_ref[...], 1.0, 0.0).astype(BF16)
        return carry

    lax.fori_loop(0, unknowns // 128, build_perm, 0)
    weighting = weights_ref[...]
    sigma = (2 * signs_ref[...] - 1).astype(F32)

    def to_faces(value, out_ref, rows):
        parts = jnp.concatenate(split3(value), axis=0)
        for f in range(4):
            moved = dot(parts, perm_ref[:, f * face : (f + 1) * face])
            out_ref[f] = moved[:rows] + moved[rows : 2 * rows] + moved[2 * rows :]

    def from_faces(in_ref, rows):
        has = (gx > 0, gx < size_x - 1, gy > 0, gy < size_y - 1)
        blocks = [jnp.where(has[f], in_ref[f], 0.0) for f in range(4)]
        parts = jnp.concatenate(split3(jnp.concatenate(blocks, axis=1)), axis=0)
        moved = dot(parts, perm_ref[...], NT)
        return moved[:rows] + moved[rows : 2 * rows] + moved[2 * rows :]

    def exchange(out_ref, in_ref, send_sem, recv_sem):
        copies = []
        for f in (3, 2, 1, 0):
            copies.append(
                pltpu.make_async_remote_copy(
                    src_ref=out_ref.at[f],
                    dst_ref=in_ref.at[opposite[f]],
                    send_sem=send_sem.at[f],
                    recv_sem=recv_sem.at[opposite[f]],
                    device_id=ways[f],
                    device_id_type=MESH,
                )
            )
        return copies

    first = loads_ref[0] * weighting
    dir_ref[...] = first
    extra = jnp.concatenate([weighting, sigma, jnp.zeros((6, unknowns), F32)], axis=0)
    to_faces(jnp.concatenate([first, extra], axis=0), first_out, cases + 8)
    pl.semaphore_wait(barrier, (plane - 1) + (depth - 1) + 4)
    copies = exchange(first_out, first_in, first_send, first_recv)
    for copy in copies:
        copy.start()

    load.wait()
    blocks = pattern_ref.shape[1]
    block_size = unknowns // blocks

    def mask_rows(i, carry):
        start = pl.multiple_of(i * block_size, block_size)
        for j in range(blocks):
            keep = jnp.where(i == j, 1, pattern_ref[0, i, j]).astype(F32)
            value = stage_ref[pl.ds(start, block_size), j * block_size : (j + 1) * block_size] * keep
            high, low = split2(value)
            zh_ref[pl.ds(start, block_size), j * block_size : (j + 1) * block_size] = high
            zl_ref[pl.ds(start, block_size), j * block_size : (j + 1) * block_size] = low
        return carry

    lax.fori_loop(0, blocks, mask_rows, 0)

    def local_product(lifted):
        high, low = split2(lifted)
        both = jnp.concatenate([high, low], axis=0)
        for n in range(4):
            tile = slice(n * face, (n + 1) * face)
            wide = dot(both, zh_ref[:, tile])
            half_ref[:, tile] = wide[:cases] + wide[cases:] + dot(high, zl_ref[:, tile])
        high, low = split2(half_ref[...])
        both = jnp.concatenate([high, low], axis=0)
        for n in range(4):
            tile = slice(n * face, (n + 1) * face)
            wide = dot(both, zh_ref[tile, :], NT)
            y_ref[:, tile] = wide[:cases] + wide[cases:] + dot(high, zl_ref[tile, :], NT)

    for copy in copies:
        copy.wait()
    moved = from_faces(first_in, cases + 8)
    wp_ref[...] = moved[cases : cases + 1]
    sgp_ref[...] = moved[cases + 1 : cases + 2]
    sg_ref[...] = sigma * sgp_ref[...] * sgp_ref[...]

    def apply(slot, lifted):
        local_product(lifted)
        to_faces(y_ref[...], halo_out.at[slot], cases)
        copies = exchange(halo_out.at[slot], halo_in.at[slot], halo_send.at[slot], halo_recv.at[slot])
        for copy in copies:
            copy.start()
        return copies

    def finish(slot, copies, out_ref, outp_ref):
        for copy in copies:
            copy.wait()
        other = from_faces(halo_in.at[slot], cases)
        out_ref[...] = y_ref[...] + 0.5 * (sgp_ref[...] * other)
        outp_ref[...] = other + 0.5 * (sg_ref[...] * y_ref[...])

    finish(0, apply(0, first + 0.5 * (sigma * moved[:cases])), img_ref, imgp_ref)
    lin_ref[...] = img_ref[...]
    linp_ref[...] = imgp_ref[...]
    res_ref[0] = loads_ref[0]
    sol_ref[0] = jnp.zeros((cases, unknowns), F32)

    def send_all(offsets, peer_of, source_of, dst_ref, send_sem, recv_sem):
        for offset in offsets:
            peer, device = peer_of(offset)
            pltpu.make_async_remote_copy(
                src_ref=source_of(peer),
                dst_ref=dst_ref,
                send_sem=send_sem,
                recv_sem=recv_sem,
                device_id=device,
                device_id_type=MESH,
            ).start()

    def stack(field, ref):
        high, low = split2(field)
        ref[: 2 * cases] = jnp.concatenate([high, high], axis=0)
        ref[2 * cases :] = jnp.concatenate([low, low], axis=0)

    def wait_bytes(ref, count, sem):
        pltpu.make_async_copy(ref.at[pl.ds(0, count)], ref.at[pl.ds(0, count)], sem).wait()

    def iteration(k, carry):
        weighted_img = weighting * img_ref[...]
        dir_high, dir_low = split2(dir_ref[...])
        win_high, win_low = split2(weighted_img)
        img_high, img_low = split2(img_ref[...])
        res_high, res_low = split2(res_ref[0])
        products = dot(
            jnp.concatenate([dir_high, win_high, dir_low, win_low], axis=0),
            jnp.concatenate([img_high, res_high, img_low, res_low], axis=0),
            NT,
        )
        both = 2 * cases
        gram = (products[:both, :both] + products[both:, both:]) + (products[:both, both:] + products[both:, :both])
        for p in range(plane):
            gram_ref[k, p] = gram[p * chunk : (p + 1) * chunk]
        send_all(plane_offsets, plane_peer, lambda peer: gram_ref.at[k, peer], scat_ref.at[k, my_plane],
                 scat_send.at[k], scat_recv.at[k])
        scat_ref[k, my_plane] = gram_ref[k, my_plane]

        @pl.when((k > 0) & (k < ITERS - 1))
        def _():
            stack(sp_ref[...], sst_ref)
            stack(imgp_ref[...], ist_ref)
            linp_ref[...] = linp_ref[...] - dot(cst_ref[:, :cases], sst_ref[...], TN)
            imgp_ref[...] = linp_ref[...] + dot(cst_ref[:, cases:], ist_ref[...], TN)

        @pl.when(k < ITERS - 1)
        def _():
            apply(k + 1, weighted_img + 0.5 * (sg_ref[...] * (wp_ref[...] * imgp_ref[...])))

        stack(dir_ref[...], dst_ref)
        stack(img_ref[...], ist_ref)
        wait_bytes(scat_ref.at[k], plane - 1, scat_recv.at[k])
        part = total([scat_ref[k, p] for p in range(plane)])
        part_ref[k, 0] = part
        line_ref[k, my_depth] = part
        send_all(line_offsets, line_peer, lambda peer: part_ref.at[k, 0], line_ref.at[k, my_depth],
                 line_send.at[k], line_recv.at[k])
        wait_bytes(line_ref.at[k], depth - 1, line_recv.at[k])
        part = total([line_ref[k, p] for p in range(depth)])
        part_ref[k, 1] = part
        gath_ref[k, my_plane] = part
        send_all(plane_offsets, plane_peer, lambda peer: part_ref.at[k, 1], gath_ref.at[k, my_plane],
                 gath_send.at[k], gath_recv.at[k])

        @pl.when(k < ITERS - 1)
        def _():
            copies = exchange(halo_out.at[k + 1], halo_in.at[k + 1], halo_send.at[k + 1], halo_recv.at[k + 1])
            finish(k + 1, copies, s_ref, sp_ref)
            stack(s_ref[...], sst_ref)

        wait_bytes(gath_ref.at[k], plane - 1, gath_recv.at[k])
        tiles = []
        for t in range(cases // 8):
            tiles.append([])
            for h in range(2):
                at = h * cases + t * 8
                pieces = [
                    gath_ref[k, row // chunk, row % chunk : row % chunk + min(chunk, 8)]
                    for row in range(at, at + 8, min(chunk, 8))
                ]
                tiles[t].append(jnp.concatenate(pieces, axis=0))
        tiles = eliminate(tiles, cases, 4)
        solved_left = jnp.concatenate([tile[0] for tile in tiles], axis=0)
        solved_right = jnp.concatenate([tile[1] for tile in tiles], axis=0)
        step_size = solved_left[:, cases:]
        update = lax.dot_general(solved_right[:, :cases], step_size, NN, precision=HIGH,
                                 preferred_element_type=F32) - solved_right[:, cases:]
        high, low = split2(jnp.concatenate([step_size, update], axis=1))
        cst_ref[...] = jnp.concatenate([high, low, high, low], axis=0)
        mixed_dir = dot(cst_ref[...], dst_ref[...], TN)
        mixed_img = dot(cst_ref[...], ist_ref[...], TN)
        sol_ref[0] = sol_ref[0] + mixed_dir[:cases]
        res_ref[0] = res_ref[0] - mixed_img[:cases]

        @pl.when(k < ITERS - 1)
        def _():
            lin_ref[...] = lin_ref[...] - dot(cst_ref[:, :cases], sst_ref[...], TN)
            dir_ref[...] = weighting * res_ref[0] + mixed_dir[cases:]
            img_ref[...] = lin_ref[...] + mixed_img[cases:]

        wait_bytes(scat_ref.at[k], plane - 1, scat_send.at[k])
        wait_bytes(line_ref.at[k], depth - 1, line_send.at[k])
        wait_bytes(gath_ref.at[k], plane - 1, gath_send.at[k])
        return carry

    lax.fori_loop(0, ITERS, iteration, 0)


def local(cfg, right_side, weights, signs, face_map, pattern, factor):
    cases, unknowns = right_side.shape[1:]
    face = unknowns // 4
    rows_y, z_lo, z_hi, cols_j, chunk = cfg
    plane, depth = rows_y * cols_j, z_lo * z_hi
    field = pltpu.VMEM((cases, unknowns), F32)
    row = pltpu.VMEM((1, unknowns), F32)
    square = pltpu.VMEM((unknowns, unknowns), BF16)
    dma = pltpu.SemaphoreType.DMA
    return pl.pallas_call(
        functools.partial(kernel, cfg),
        out_shape=(jax.ShapeDtypeStruct(right_side.shape, F32),) * 2,
        in_specs=[pl.BlockSpec(memory_space=pltpu.VMEM)] * 4
        + [pl.BlockSpec(memory_space=pltpu.SMEM), pl.BlockSpec(memory_space=pl.ANY)],
        out_specs=(pl.BlockSpec(memory_space=pltpu.VMEM),) * 2,
        scratch_shapes=[
            pltpu.VMEM((unknowns, unknowns), F32), square, square, square,
            field, field, field, field, field, field, field,
            pltpu.VMEM((4 * cases, unknowns), BF16), pltpu.VMEM((4 * cases, unknowns), BF16),
            pltpu.VMEM((4 * cases, unknowns), BF16), pltpu.VMEM((4 * cases, 2 * cases), BF16),
            field, field, row, row, row,
            pltpu.VMEM((4, cases + 8, face), F32), pltpu.VMEM((4, cases + 8, face), F32),
            pltpu.VMEM((ITERS, 4, cases, face), F32), pltpu.VMEM((ITERS, 4, cases, face), F32),
            pltpu.VMEM((ITERS, plane, chunk, 128), F32), pltpu.VMEM((ITERS, plane, chunk, 128), F32),
            pltpu.VMEM((ITERS, 2, chunk, 128), F32), pltpu.VMEM((ITERS, depth, chunk, 128), F32),
            pltpu.VMEM((ITERS, plane, chunk, 128), F32),
            dma, dma((4,)), dma((4,)), dma((ITERS, 4)), dma((ITERS, 4)),
            dma((ITERS,)), dma((ITERS,)), dma((ITERS,)), dma((ITERS,)), dma((ITERS,)), dma((ITERS,)),
        ],
        compiler_params=pltpu.CompilerParams(
            collective_id=0, has_side_effects=True, vmem_limit_bytes=60 * 1024 * 1024
        ),
    )(right_side, weights, signs, face_map, pattern, factor)


def solution(mesh):
    size_x, size_y = mesh.shape["gx"], mesh.shape["gy"]
    z_lo = min(Z_PARTS, size_x // 2)
    z_hi = min(Z_PARTS, size_y // 2)
    rows_y, cols_j = size_x // z_lo, size_y // z_hi
    chunk = 128 // (rows_y * cols_j)
    return jax.shard_map(
        functools.partial(local, (rows_y, z_lo, z_hi, cols_j, chunk)),
        mesh=mesh,
        in_specs=(
            P("gx", None, "gy"),
            P("gx", "gy"),
            P("gx", "gy"),
            P("gx", "gy"),
            P("gx", None, "gy"),
            P("gx", None, "gy"),
        ),
        out_specs=(P("gx", None, "gy"), P("gx", None, "gy")),
        check_vma=False,
    )
```

```python
import functools

import jax
import jax.numpy as jnp
from jax import lax
from jax.experimental import pallas as pl
from jax.experimental.pallas import tpu as pltpu
from jax.sharding import PartitionSpec as P

ITERS = 4
MESH = pl.DeviceIdType.MESH
HIGH = lax.Precision.HIGHEST
F32 = jnp.float32
BF16 = jnp.bfloat16
NN = (((1,), (0,)), ((), ()))
NT = (((1,), (1,)), ((), ()))
TN = (((0,), (0,)), ((), ()))
SENT_ORDER = (3, 2, 1, 0)
Z_PARTS = 4


def split2(value):
    high = value.astype(BF16)
    low = (value - high.astype(F32)).astype(BF16)
    return high, low


def split3(value):
    high = value.astype(BF16)
    rest = value - high.astype(F32)
    middle = rest.astype(BF16)
    low = (rest - middle.astype(F32)).astype(BF16)
    return high, middle, low


def dot(left, right, dims=NN):
    return lax.dot_general(left, right, dims, preferred_element_type=F32)


def invert_small(entries):
    count = len(entries)
    rows = [list(row) + [None] * count for row in entries]
    work = [[entries[r][c] for c in range(count)] for r in range(count)]
    inverse = [[None] * count for _ in range(count)]
    for pivot in range(count):
        scale = 1.0 / work[pivot][pivot]
        for c in range(count):
            if c > pivot:
                work[pivot][c] = work[pivot][c] * scale
            if c < pivot:
                inverse[pivot][c] = inverse[pivot][c] * scale
        inverse[pivot][pivot] = scale
        for r in range(count):
            if r == pivot:
                continue
            factor = work[r][pivot]
            for c in range(count):
                if c > pivot:
                    work[r][c] = work[r][c] - factor * work[pivot][c]
                if c < pivot:
                    inverse[r][c] = inverse[r][c] - factor * inverse[pivot][c]
            inverse[r][pivot] = -factor * scale
    return inverse


def total(terms):
    while len(terms) > 1:
        terms = [terms[i] + terms[i + 1] if i + 1 < len(terms) else terms[i] for i in range(0, len(terms), 2)]
    return terms[0]


def eliminate(tiles, size, block):
    wide = len(tiles[0])
    sublane = lax.broadcasted_iota(jnp.int32, (8, 128), 0)

    def lane(tile, at):
        return jnp.broadcast_to(tile[:, at : at + 1], (8, 128))

    def row(tile, at):
        return jnp.broadcast_to(tile[at : at + 1, :], (8, 128))

    columns = [[lane(tile[0], r) for tile in tiles] for r in range(block)]
    for start in range(0, size, block):
        home, first = start // 8, start % 8
        span = range(block)
        ahead = start + block < size
        before = [[lane(tile[0], start + block + r) for tile in tiles] for r in span] if ahead else []
        inverse = invert_small([[row(columns[c][home], first + r) for c in span] for r in span])

        def eliminated(values, lines):
            scaled = [total([inverse[r][c] * lines[c] for c in span]) for r in span]
            out = []
            for t, value in enumerate(values):
                new = value - total([columns[r][t] * scaled[r] for r in span])
                if t == home:
                    for r in span:
                        new = jnp.where(sublane == first + r, scaled[r], new)
                out.append(new)
            return out

        following = [eliminated(b, [row(b[home], first + c) for c in span]) for b in before]
        for h in range(wide):
            done = eliminated([tile[h] for tile in tiles], [row(tiles[home][h], first + c) for c in span])
            for t, value in enumerate(done):
                tiles[t][h] = value
        columns = following
    return tiles


def ring(offset, count):
    return min(offset, count - offset)


def kernel(
    cfg,
    loads_ref, weights_ref, signs_ref, map_ref, pattern_ref, factor_hbm,
    sol_ref, res_ref,
    stage_ref, zh_ref, zl_ref, perm_ref, dir_ref, img_ref, imgp_ref, lin_ref, linp_ref, s_ref, sp_ref,
    dst_ref, ist_ref, sst_ref, cst_ref, half_ref, y_ref, wp_ref, sg_ref, sgp_ref, first_out, first_in, halo_out, halo_in,
    gram_ref, scat_ref, part_ref, line_ref, gath_ref,
    load_sem, first_send, first_recv, halo_send, halo_recv,
    scat_send, scat_recv, line_send, line_recv, gath_send, gath_recv,
):
    rows_y, z_lo, z_hi, cols_j, chunk = cfg
    plane, depth = rows_y * cols_j, z_lo * z_hi
    gx, gy = lax.axis_index("gx"), lax.axis_index("gy")
    size_x, size_y = rows_y * z_lo, z_hi * cols_j
    my_y, my_lo = gx // z_lo, gx % z_lo
    my_hi, my_j = gy // cols_j, gy % cols_j
    my_plane = my_y * cols_j + my_j
    my_depth = my_hi * z_lo + my_lo
    cases, unknowns = loads_ref.shape[1], loads_ref.shape[2]
    face = unknowns // 4
    north = ((gx + size_x - 1) % size_x, gy)
    south = ((gx + 1) % size_x, gy)
    west = (gx, (gy + size_y - 1) % size_y)
    east = (gx, (gy + 1) % size_y)
    ways = (north, south, west, east)
    opposite = (1, 0, 3, 2)

    def plane_peer(offset):
        peer_y = (my_y + offset[0]) % rows_y
        peer_j = ((my_j // 2 + offset[1]) % (cols_j // 2)) * 2 + (my_j + offset[2]) % 2
        return peer_y * cols_j + peer_j, (peer_y * z_lo + my_lo, my_hi * cols_j + peer_j)

    def line_peer(offset):
        peer = (my_depth + offset) % depth
        return peer, (my_y * z_lo + peer % z_lo, (peer // z_lo) * cols_j + my_j)

    plane_offsets = sorted(
        [(a, b, c) for a in range(rows_y) for b in range(cols_j // 2) for c in range(2) if a or b or c],
        key=lambda o: -(ring(o[0], rows_y) + ring(o[1], cols_j // 2) + 0.5 * o[2]),
    )
    line_offsets = sorted(range(1, depth), key=lambda o: -ring(o, depth))

    load = pltpu.make_async_copy(factor_hbm.at[0], stage_ref, load_sem)
    load.start()

    barrier = pltpu.get_barrier_semaphore()

    def signal(device):
        pl.semaphore_signal(barrier, inc=1, device_id=device, device_id_type=MESH)

    for offset in line_offsets:
        signal(line_peer(offset)[1])
    for way in ways:
        signal(way)
    for offset in plane_offsets:
        signal(plane_peer(offset)[1])

    def build_perm(f):
        columns = slice(f * face, (f + 1) * face)

        def body(step, carry):
            start = pl.multiple_of(step * 128, 128)
            index = lax.broadcasted_iota(jnp.int32, (128, face), 0) + step * 128
            perm_ref[pl.ds(start, 128), columns] = jnp.where(index == map_ref[:, columns], 1.0, 0.0).astype(BF16)
            return carry

        lax.fori_loop(0, unknowns // 128, body, 0)

    weighting = weights_ref[...]
    sigma = (2 * signs_ref[...] - 1).astype(F32)

    def to_faces(value, out_ref, rows, before=lambda f: None, after=lambda f: None):
        parts = jnp.concatenate(split3(value), axis=0)
        for f in SENT_ORDER:
            before(f)
            moved = dot(parts, perm_ref[:, f * face : (f + 1) * face])
            out_ref[f] = moved[:rows] + moved[rows : 2 * rows] + moved[2 * rows :]
            after(f)

    def from_faces(in_ref, rows):
        has = (gx > 0, gx < size_x - 1, gy > 0, gy < size_y - 1)
        blocks = [jnp.where(has[f], in_ref[f], 0.0) for f in range(4)]
        parts = jnp.concatenate(split3(jnp.concatenate(blocks, axis=1)), axis=0)
        moved = dot(parts, perm_ref[...], NT)
        return moved[:rows] + moved[rows : 2 * rows] + moved[2 * rows :]

    def exchange(out_ref, in_ref, send_sem, recv_sem):
        return {
            f: pltpu.make_async_remote_copy(
                src_ref=out_ref.at[f],
                dst_ref=in_ref.at[opposite[f]],
                send_sem=send_sem.at[f],
                recv_sem=recv_sem.at[opposite[f]],
                device_id=ways[f],
                device_id_type=MESH,
            )
            for f in SENT_ORDER
        }

    def halo(slot):
        return exchange(halo_out.at[slot], halo_in.at[slot], halo_send.at[slot], halo_recv.at[slot])

    first = loads_ref[0] * weighting
    dir_ref[...] = first
    extra = jnp.concatenate([weighting, sigma, jnp.zeros((6, unknowns), F32)], axis=0)
    copies = exchange(first_out, first_in, first_send, first_recv)

    def start_first(f):
        if f == SENT_ORDER[0]:
            pl.semaphore_wait(barrier, (plane - 1) + (depth - 1) + 4)
        copies[f].start()

    to_faces(jnp.concatenate([first, extra], axis=0), first_out, cases + 8, build_perm, start_first)

    load.wait()
    blocks = pattern_ref.shape[1]
    block_size = unknowns // blocks

    def mask_rows(i, carry):
        start = pl.multiple_of(i * block_size, block_size)
        for j in range(blocks):
            keep = jnp.where(i == j, 1, pattern_ref[0, i, j]).astype(F32)
            value = stage_ref[pl.ds(start, block_size), j * block_size : (j + 1) * block_size] * keep
            high, low = split2(value)
            zh_ref[pl.ds(start, block_size), j * block_size : (j + 1) * block_size] = high
            zl_ref[pl.ds(start, block_size), j * block_size : (j + 1) * block_size] = low
        return carry

    lax.fori_loop(0, blocks, mask_rows, 0)

    def local_product(lifted):
        high, low = split2(lifted)
        both = jnp.concatenate([high, low], axis=0)
        for n in range(4):
            tile = slice(n * face, (n + 1) * face)
            wide = dot(both, zh_ref[:, tile])
            half_ref[:, tile] = wide[:cases] + wide[cases:] + dot(high, zl_ref[:, tile])
        high, low = split2(half_ref[...])
        both = jnp.concatenate([high, low], axis=0)
        for n in range(4):
            tile = slice(n * face, (n + 1) * face)
            wide = dot(both, zh_ref[tile, :], NT)
            y_ref[:, tile] = wide[:cases] + wide[cases:] + dot(high, zl_ref[tile, :], NT)

    for copy in copies.values():
        copy.wait()
    moved = from_faces(first_in, cases + 8)
    wp_ref[...] = moved[cases : cases + 1]
    sgp_ref[...] = moved[cases + 1 : cases + 2]
    sg_ref[...] = sigma * sgp_ref[...] * sgp_ref[...]

    def finish(slot, out_ref, outp_ref):
        for copy in halo(slot).values():
            copy.wait()
        other = from_faces(halo_in.at[slot], cases)
        out_ref[...] = y_ref[...] + 0.5 * (sgp_ref[...] * other)
        outp_ref[...] = other + 0.5 * (sg_ref[...] * y_ref[...])

    local_product(first + 0.5 * (sigma * moved[:cases]))
    copies = halo(0)
    to_faces(y_ref[...], halo_out.at[0], cases, after=lambda f: copies[f].start())
    finish(0, img_ref, imgp_ref)
    lin_ref[...] = img_ref[...]
    linp_ref[...] = imgp_ref[...]
    res_ref[0] = loads_ref[0]
    sol_ref[0] = jnp.zeros((cases, unknowns), F32)

    def send_all(offsets, peer_of, source_of, dst_ref, send_sem, recv_sem):
        for offset in offsets:
            peer, device = peer_of(offset)
            pltpu.make_async_remote_copy(
                src_ref=source_of(peer),
                dst_ref=dst_ref,
                send_sem=send_sem,
                recv_sem=recv_sem,
                device_id=device,
                device_id_type=MESH,
            ).start()

    def stack(field, ref):
        high, low = split2(field)
        ref[: 2 * cases] = jnp.concatenate([high, high], axis=0)
        ref[2 * cases :] = jnp.concatenate([low, low], axis=0)

    def wait_bytes(ref, count, sem):
        pltpu.make_async_copy(ref.at[pl.ds(0, count)], ref.at[pl.ds(0, count)], sem).wait()

    def iteration(k, carry):
        weighted_img = weighting * img_ref[...]
        dir_high, dir_low = split2(dir_ref[...])
        win_high, win_low = split2(weighted_img)
        img_high, img_low = split2(img_ref[...])
        res_high, res_low = split2(res_ref[0])
        products = dot(
            jnp.concatenate([dir_high, win_high, dir_low, win_low], axis=0),
            jnp.concatenate([img_high, res_high, img_low, res_low], axis=0),
            NT,
        )
        both = 2 * cases
        gram = (products[:both, :both] + products[both:, both:]) + (products[:both, both:] + products[both:, :both])
        for p in range(plane):
            gram_ref[k, p] = gram[p * chunk : (p + 1) * chunk]
        send_all(plane_offsets, plane_peer, lambda peer: gram_ref.at[k, peer], scat_ref.at[k, my_plane],
                 scat_send.at[k], scat_recv.at[k])
        scat_ref[k, my_plane] = gram_ref[k, my_plane]

        @pl.when((k > 0) & (k < ITERS - 1))
        def _():
            stack(sp_ref[...], sst_ref)
            stack(imgp_ref[...], ist_ref)
            linp_ref[...] = linp_ref[...] - dot(cst_ref[:, :cases], sst_ref[...], TN)
            imgp_ref[...] = linp_ref[...] + dot(cst_ref[:, cases:], ist_ref[...], TN)

        @pl.when(k < ITERS - 1)
        def _():
            local_product(weighted_img + 0.5 * (sg_ref[...] * (wp_ref[...] * imgp_ref[...])))
            to_faces(y_ref[...], halo_out.at[k + 1], cases)

        stack(dir_ref[...], dst_ref)
        stack(img_ref[...], ist_ref)
        wait_bytes(scat_ref.at[k], plane - 1, scat_recv.at[k])
        part = total([scat_ref[k, p] for p in range(plane)])
        part_ref[k, 0] = part
        line_ref[k, my_depth] = part
        send_all(line_offsets, line_peer, lambda peer: part_ref.at[k, 0], line_ref.at[k, my_depth],
                 line_send.at[k], line_recv.at[k])

        @pl.when(k < ITERS - 1)
        def _():
            for copy in halo(k + 1).values():
                copy.start()

        wait_bytes(line_ref.at[k], depth - 1, line_recv.at[k])
        part = total([line_ref[k, p] for p in range(depth)])
        part_ref[k, 1] = part
        gath_ref[k, my_plane] = part
        send_all(plane_offsets, plane_peer, lambda peer: part_ref.at[k, 1], gath_ref.at[k, my_plane],
                 gath_send.at[k], gath_recv.at[k])

        @pl.when(k < ITERS - 1)
        def _():
            finish(k + 1, s_ref, sp_ref)
            stack(s_ref[...], sst_ref)

        wait_bytes(gath_ref.at[k], plane - 1, gath_recv.at[k])
        tiles = []
        for t in range(cases // 8):
            tiles.append([])
            for h in range(2):
                at = h * cases + t * 8
                pieces = [
                    gath_ref[k, row // chunk, row % chunk : row % chunk + min(chunk, 8)]
                    for row in range(at, at + 8, min(chunk, 8))
                ]
                tiles[t].append(jnp.concatenate(pieces, axis=0))
        tiles = eliminate(tiles, cases, 4)
        solved_left = jnp.concatenate([tile[0] for tile in tiles], axis=0)
        solved_right = jnp.concatenate([tile[1] for tile in tiles], axis=0)
        step_size = solved_left[:, cases:]
        update = lax.dot_general(solved_right[:, :cases], step_size, NN, precision=HIGH,
                                 preferred_element_type=F32) - solved_right[:, cases:]
        high, low = split2(jnp.concatenate([step_size, update], axis=1))
        cst_ref[...] = jnp.concatenate([high, low, high, low], axis=0)
        mixed_dir = dot(cst_ref[...], dst_ref[...], TN)
        mixed_img = dot(cst_ref[...], ist_ref[...], TN)
        sol_ref[0] = sol_ref[0] + mixed_dir[:cases]
        res_ref[0] = res_ref[0] - mixed_img[:cases]

        @pl.when(k < ITERS - 1)
        def _():
            lin_ref[...] = lin_ref[...] - dot(cst_ref[:, :cases], sst_ref[...], TN)
            dir_ref[...] = weighting * res_ref[0] + mixed_dir[cases:]
            img_ref[...] = lin_ref[...] + mixed_img[cases:]

        wait_bytes(scat_ref.at[k], plane - 1, scat_send.at[k])
        wait_bytes(line_ref.at[k], depth - 1, line_send.at[k])
        wait_bytes(gath_ref.at[k], plane - 1, gath_send.at[k])
        return carry

    lax.fori_loop(0, ITERS, iteration, 0)


def store(sol_in, res_in, sol_out, res_out, sol_held, res_held, read_sem, write_sem):
    held = (sol_held, res_held)
    reads = [pltpu.make_async_copy(v, held[i], read_sem.at[i]) for i, v in enumerate((sol_in, res_in))]
    writes = [pltpu.make_async_copy(held[i], v, write_sem.at[i]) for i, v in enumerate((sol_out, res_out))]
    for read in reads:
        read.start()
    for read, write in zip(reads, writes):
        read.wait()
        write.start()
    for write in writes:
        write.wait()


def local(cfg, right_side, weights, signs, face_map, pattern, factor):
    cases, unknowns = right_side.shape[1:]
    face = unknowns // 4
    rows_y, z_lo, z_hi, cols_j, chunk = cfg
    plane, depth = rows_y * cols_j, z_lo * z_hi
    field = pltpu.VMEM((cases, unknowns), F32)
    row = pltpu.VMEM((1, unknowns), F32)
    square = pltpu.VMEM((unknowns, unknowns), BF16)
    dma = pltpu.SemaphoreType.DMA
    results = pl.pallas_call(
        functools.partial(kernel, cfg),
        out_shape=(jax.ShapeDtypeStruct(right_side.shape, F32),) * 2,
        in_specs=[pl.BlockSpec(memory_space=pltpu.VMEM)] * 4
        + [pl.BlockSpec(memory_space=pltpu.SMEM), pl.BlockSpec(memory_space=pl.ANY)],
        out_specs=(pl.BlockSpec(memory_space=pltpu.VMEM),) * 2,
        scratch_shapes=[
            pltpu.VMEM((unknowns, unknowns), F32), square, square, square,
            field, field, field, field, field, field, field,
            pltpu.VMEM((4 * cases, unknowns), BF16), pltpu.VMEM((4 * cases, unknowns), BF16),
            pltpu.VMEM((4 * cases, unknowns), BF16), pltpu.VMEM((4 * cases, 2 * cases), BF16),
            field, field, row, row, row,
            pltpu.VMEM((4, cases + 8, face), F32), pltpu.VMEM((4, cases + 8, face), F32),
            pltpu.VMEM((ITERS, 4, cases, face), F32), pltpu.VMEM((ITERS, 4, cases, face), F32),
            pltpu.VMEM((ITERS, plane, chunk, 128), F32), pltpu.VMEM((ITERS, plane, chunk, 128), F32),
            pltpu.VMEM((ITERS, 2, chunk, 128), F32), pltpu.VMEM((ITERS, depth, chunk, 128), F32),
            pltpu.VMEM((ITERS, plane, chunk, 128), F32),
            dma, dma((4,)), dma((4,)), dma((ITERS, 4)), dma((ITERS, 4)),
            dma((ITERS,)), dma((ITERS,)), dma((ITERS,)), dma((ITERS,)), dma((ITERS,)), dma((ITERS,)),
        ],
        compiler_params=pltpu.CompilerParams(
            collective_id=0, has_side_effects=True, vmem_limit_bytes=60 * 1024 * 1024
        ),
    )(right_side, weights, signs, face_map, pattern, factor)
    return pl.pallas_call(
        store,
        out_shape=(jax.ShapeDtypeStruct(right_side.shape, F32),) * 2,
        in_specs=[pl.BlockSpec(memory_space=pl.ANY)] * 2,
        out_specs=(pl.BlockSpec(memory_space=pl.ANY),) * 2,
        scratch_shapes=[pltpu.VMEM(right_side.shape, F32)] * 2 + [dma((2,))] * 2,
    )(*results)


def solution(mesh):
    size_x, size_y = mesh.shape["gx"], mesh.shape["gy"]
    z_lo = min(Z_PARTS, size_x // 2)
    z_hi = min(Z_PARTS, size_y // 2)
    rows_y, cols_j = size_x // z_lo, size_y // z_hi
    chunk = 128 // (rows_y * cols_j)
    return jax.shard_map(
        functools.partial(local, (rows_y, z_lo, z_hi, cols_j, chunk)),
        mesh=mesh,
        in_specs=(
            P("gx", None, "gy"),
            P("gx", "gy"),
            P("gx", "gy"),
            P("gx", "gy"),
            P("gx", None, "gy"),
            P("gx", None, "gy"),
        ),
        out_specs=(P("gx", None, "gy"), P("gx", None, "gy")),
        check_vma=False,
    )
```

```python
import functools

import jax
import jax.numpy as jnp
from jax import lax
from jax.experimental import pallas as pl
from jax.experimental.pallas import tpu as pltpu
from jax.sharding import PartitionSpec as P

ITERS = 4
MESH = pl.DeviceIdType.MESH
HIGH = lax.Precision.HIGHEST
F32 = jnp.float32
BF16 = jnp.bfloat16
NN = (((1,), (0,)), ((), ()))
NT = (((1,), (1,)), ((), ()))
TN = (((0,), (0,)), ((), ()))
SENT_ORDER = (3, 2, 1, 0)
Z_PARTS = 4


def split2(value):
    high = value.astype(BF16)
    low = (value - high.astype(F32)).astype(BF16)
    return high, low


def split3(value):
    high = value.astype(BF16)
    rest = value - high.astype(F32)
    middle = rest.astype(BF16)
    low = (rest - middle.astype(F32)).astype(BF16)
    return high, middle, low


def dot(left, right, dims=NN):
    return lax.dot_general(left, right, dims, preferred_element_type=F32)


def invert_small(entries):
    count = len(entries)
    rows = [list(row) + [None] * count for row in entries]
    work = [[entries[r][c] for c in range(count)] for r in range(count)]
    inverse = [[None] * count for _ in range(count)]
    for pivot in range(count):
        scale = 1.0 / work[pivot][pivot]
        for c in range(count):
            if c > pivot:
                work[pivot][c] = work[pivot][c] * scale
            if c < pivot:
                inverse[pivot][c] = inverse[pivot][c] * scale
        inverse[pivot][pivot] = scale
        for r in range(count):
            if r == pivot:
                continue
            factor = work[r][pivot]
            for c in range(count):
                if c > pivot:
                    work[r][c] = work[r][c] - factor * work[pivot][c]
                if c < pivot:
                    inverse[r][c] = inverse[r][c] - factor * inverse[pivot][c]
            inverse[r][pivot] = -factor * scale
    return inverse


def total(terms):
    while len(terms) > 1:
        terms = [terms[i] + terms[i + 1] if i + 1 < len(terms) else terms[i] for i in range(0, len(terms), 2)]
    return terms[0]


def eliminate(tiles, size, block):
    wide = len(tiles[0])
    sublane = lax.broadcasted_iota(jnp.int32, (8, 128), 0)

    def lane(tile, at):
        return jnp.broadcast_to(tile[:, at : at + 1], (8, 128))

    def row(tile, at):
        return jnp.broadcast_to(tile[at : at + 1, :], (8, 128))

    columns = [[lane(tile[0], r) for tile in tiles] for r in range(block)]
    for start in range(0, size, block):
        home, first = start // 8, start % 8
        span = range(block)
        ahead = start + block < size
        before = [[lane(tile[0], start + block + r) for tile in tiles] for r in span] if ahead else []
        inverse = invert_small([[row(columns[c][home], first + r) for c in span] for r in span])

        def eliminated(values, lines):
            scaled = [total([inverse[r][c] * lines[c] for c in span]) for r in span]
            out = []
            for t, value in enumerate(values):
                new = value - total([columns[r][t] * scaled[r] for r in span])
                if t == home:
                    for r in span:
                        new = jnp.where(sublane == first + r, scaled[r], new)
                out.append(new)
            return out

        following = [eliminated(b, [row(b[home], first + c) for c in span]) for b in before]
        for h in range(wide):
            done = eliminated([tile[h] for tile in tiles], [row(tiles[home][h], first + c) for c in span])
            for t, value in enumerate(done):
                tiles[t][h] = value
        columns = following
    return tiles


def ring(offset, count):
    return min(offset, count - offset)


def kernel(
    cfg,
    loads_hbm, weights_ref, signs_ref, map_ref, pattern_ref, factor_hbm,
    sol_ref, res_ref,
    loads_ref, stage_ref, zh_ref, zl_ref, perm_ref, dir_ref, img_ref, imgp_ref, lin_ref, linp_ref, s_ref, sp_ref,
    dst_ref, ist_ref, sst_ref, cst_ref, half_ref, y_ref, wp_ref, sg_ref, sgp_ref, first_out, first_in, halo_out, halo_in,
    gram_ref, scat_ref, part_ref, line_ref, gath_ref,
    loads_sem, load_sem, first_send, first_recv, halo_send, halo_recv,
    scat_send, scat_recv, line_send, line_recv, gath_send, gath_recv,
):
    rows_y, z_lo, z_hi, cols_j, chunk = cfg
    plane, depth = rows_y * cols_j, z_lo * z_hi
    gx, gy = lax.axis_index("gx"), lax.axis_index("gy")
    size_x, size_y = rows_y * z_lo, z_hi * cols_j
    my_y, my_lo = gx // z_lo, gx % z_lo
    my_hi, my_j = gy // cols_j, gy % cols_j
    my_plane = my_y * cols_j + my_j
    my_depth = my_hi * z_lo + my_lo
    cases, unknowns = loads_ref.shape[1], loads_ref.shape[2]
    face = unknowns // 4
    north = ((gx + size_x - 1) % size_x, gy)
    south = ((gx + 1) % size_x, gy)
    west = (gx, (gy + size_y - 1) % size_y)
    east = (gx, (gy + 1) % size_y)
    ways = (north, south, west, east)
    opposite = (1, 0, 3, 2)

    def plane_peer(offset):
        peer_y = (my_y + offset[0]) % rows_y
        peer_j = ((my_j // 2 + offset[1]) % (cols_j // 2)) * 2 + (my_j + offset[2]) % 2
        return peer_y * cols_j + peer_j, (peer_y * z_lo + my_lo, my_hi * cols_j + peer_j)

    def line_peer(offset):
        peer = (my_depth + offset) % depth
        return peer, (my_y * z_lo + peer % z_lo, (peer // z_lo) * cols_j + my_j)

    plane_offsets = sorted(
        [(a, b, c) for a in range(rows_y) for b in range(cols_j // 2) for c in range(2) if a or b or c],
        key=lambda o: -(ring(o[0], rows_y) + ring(o[1], cols_j // 2) + 0.5 * o[2]),
    )
    line_offsets = sorted(range(1, depth), key=lambda o: -ring(o, depth))

    loads = pltpu.make_async_copy(loads_hbm, loads_ref, loads_sem)
    loads.start()
    load = pltpu.make_async_copy(factor_hbm.at[0], stage_ref, load_sem)
    load.start()

    barrier = pltpu.get_barrier_semaphore()

    def signal(device):
        pl.semaphore_signal(barrier, inc=1, device_id=device, device_id_type=MESH)

    for offset in line_offsets:
        signal(line_peer(offset)[1])
    for way in ways:
        signal(way)
    for offset in plane_offsets:
        signal(plane_peer(offset)[1])

    def build_perm(f):
        columns = slice(f * face, (f + 1) * face)

        def body(step, carry):
            start = pl.multiple_of(step * 128, 128)
            index = lax.broadcasted_iota(jnp.int32, (128, face), 0) + step * 128
            perm_ref[pl.ds(start, 128), columns] = jnp.where(index == map_ref[:, columns], 1.0, 0.0).astype(BF16)
            return carry

        lax.fori_loop(0, unknowns // 128, body, 0)

    weighting = weights_ref[...]
    sigma = (2 * signs_ref[...] - 1).astype(F32)

    def to_faces(value, out_ref, rows, before=lambda f: None, after=lambda f: None):
        parts = jnp.concatenate(split3(value), axis=0)
        for f in SENT_ORDER:
            before(f)
            moved = dot(parts, perm_ref[:, f * face : (f + 1) * face])
            out_ref[f] = moved[:rows] + moved[rows : 2 * rows] + moved[2 * rows :]
            after(f)

    def from_faces(in_ref, rows):
        has = (gx > 0, gx < size_x - 1, gy > 0, gy < size_y - 1)
        blocks = [jnp.where(has[f], in_ref[f], 0.0) for f in range(4)]
        parts = jnp.concatenate(split3(jnp.concatenate(blocks, axis=1)), axis=0)
        moved = dot(parts, perm_ref[...], NT)
        return moved[:rows] + moved[rows : 2 * rows] + moved[2 * rows :]

    def exchange(out_ref, in_ref, send_sem, recv_sem):
        return {
            f: pltpu.make_async_remote_copy(
                src_ref=out_ref.at[f],
                dst_ref=in_ref.at[opposite[f]],
                send_sem=send_sem.at[f],
                recv_sem=recv_sem.at[opposite[f]],
                device_id=ways[f],
                device_id_type=MESH,
            )
            for f in SENT_ORDER
        }

    def halo(slot):
        return exchange(halo_out.at[slot], halo_in.at[slot], halo_send.at[slot], halo_recv.at[slot])

    loads.wait()
    first = loads_ref[0] * weighting
    dir_ref[...] = first
    extra = jnp.concatenate([weighting, sigma, jnp.zeros((6, unknowns), F32)], axis=0)
    copies = exchange(first_out, first_in, first_send, first_recv)

    def start_first(f):
        if f == SENT_ORDER[0]:
            pl.semaphore_wait(barrier, (plane - 1) + (depth - 1) + 4)
        copies[f].start()

    to_faces(jnp.concatenate([first, extra], axis=0), first_out, cases + 8, build_perm, start_first)

    load.wait()
    blocks = pattern_ref.shape[1]
    block_size = unknowns // blocks

    def mask_rows(i, carry):
        start = pl.multiple_of(i * block_size, block_size)
        for j in range(blocks):
            keep = jnp.where(i == j, 1, pattern_ref[0, i, j]).astype(F32)
            value = stage_ref[pl.ds(start, block_size), j * block_size : (j + 1) * block_size] * keep
            high, low = split2(value)
            zh_ref[pl.ds(start, block_size), j * block_size : (j + 1) * block_size] = high
            zl_ref[pl.ds(start, block_size), j * block_size : (j + 1) * block_size] = low
        return carry

    lax.fori_loop(0, blocks, mask_rows, 0)

    def local_product(lifted):
        high, low = split2(lifted)
        both = jnp.concatenate([high, low], axis=0)
        for n in range(4):
            tile = slice(n * face, (n + 1) * face)
            wide = dot(both, zh_ref[:, tile])
            half_ref[:, tile] = wide[:cases] + wide[cases:] + dot(high, zl_ref[:, tile])
        high, low = split2(half_ref[...])
        both = jnp.concatenate([high, low], axis=0)
        for n in range(4):
            tile = slice(n * face, (n + 1) * face)
            wide = dot(both, zh_ref[tile, :], NT)
            y_ref[:, tile] = wide[:cases] + wide[cases:] + dot(high, zl_ref[tile, :], NT)

    for copy in copies.values():
        copy.wait()
    moved = from_faces(first_in, cases + 8)
    wp_ref[...] = moved[cases : cases + 1]
    sgp_ref[...] = moved[cases + 1 : cases + 2]
    sg_ref[...] = sigma * sgp_ref[...] * sgp_ref[...]

    def finish(slot, out_ref, outp_ref):
        for copy in halo(slot).values():
            copy.wait()
        other = from_faces(halo_in.at[slot], cases)
        out_ref[...] = y_ref[...] + 0.5 * (sgp_ref[...] * other)
        outp_ref[...] = other + 0.5 * (sg_ref[...] * y_ref[...])

    local_product(first + 0.5 * (sigma * moved[:cases]))
    copies = halo(0)
    to_faces(y_ref[...], halo_out.at[0], cases, after=lambda f: copies[f].start())
    finish(0, img_ref, imgp_ref)
    lin_ref[...] = img_ref[...]
    linp_ref[...] = imgp_ref[...]
    res_ref[0] = loads_ref[0]
    sol_ref[0] = jnp.zeros((cases, unknowns), F32)

    def send_all(offsets, peer_of, source_of, dst_ref, send_sem, recv_sem):
        for offset in offsets:
            peer, device = peer_of(offset)
            pltpu.make_async_remote_copy(
                src_ref=source_of(peer),
                dst_ref=dst_ref,
                send_sem=send_sem,
                recv_sem=recv_sem,
                device_id=device,
                device_id_type=MESH,
            ).start()

    def stack(field, ref):
        high, low = split2(field)
        ref[: 2 * cases] = jnp.concatenate([high, high], axis=0)
        ref[2 * cases :] = jnp.concatenate([low, low], axis=0)

    def wait_bytes(ref, count, sem):
        pltpu.make_async_copy(ref.at[pl.ds(0, count)], ref.at[pl.ds(0, count)], sem).wait()

    def iteration(k, carry):
        weighted_img = weighting * img_ref[...]
        dir_high, dir_low = split2(dir_ref[...])
        win_high, win_low = split2(weighted_img)
        img_high, img_low = split2(img_ref[...])
        res_high, res_low = split2(res_ref[0])
        products = dot(
            jnp.concatenate([dir_high, win_high, dir_low, win_low], axis=0),
            jnp.concatenate([img_high, res_high, img_low, res_low], axis=0),
            NT,
        )
        both = 2 * cases
        gram = (products[:both, :both] + products[both:, both:]) + (products[:both, both:] + products[both:, :both])
        for p in range(plane):
            gram_ref[k, p] = gram[p * chunk : (p + 1) * chunk]
        send_all(plane_offsets, plane_peer, lambda peer: gram_ref.at[k, peer], scat_ref.at[k, my_plane],
                 scat_send.at[k], scat_recv.at[k])
        scat_ref[k, my_plane] = gram_ref[k, my_plane]

        @pl.when((k > 0) & (k < ITERS - 1))
        def _():
            stack(sp_ref[...], sst_ref)
            stack(imgp_ref[...], ist_ref)
            linp_ref[...] = linp_ref[...] - dot(cst_ref[:, :cases], sst_ref[...], TN)
            imgp_ref[...] = linp_ref[...] + dot(cst_ref[:, cases:], ist_ref[...], TN)

        @pl.when(k < ITERS - 1)
        def _():
            local_product(weighted_img + 0.5 * (sg_ref[...] * (wp_ref[...] * imgp_ref[...])))
            to_faces(y_ref[...], halo_out.at[k + 1], cases)

        stack(dir_ref[...], dst_ref)
        stack(img_ref[...], ist_ref)
        wait_bytes(scat_ref.at[k], plane - 1, scat_recv.at[k])
        part = total([scat_ref[k, p] for p in range(plane)])
        part_ref[k, 0] = part
        line_ref[k, my_depth] = part
        send_all(line_offsets, line_peer, lambda peer: part_ref.at[k, 0], line_ref.at[k, my_depth],
                 line_send.at[k], line_recv.at[k])

        @pl.when(k < ITERS - 1)
        def _():
            for copy in halo(k + 1).values():
                copy.start()

        wait_bytes(line_ref.at[k], depth - 1, line_recv.at[k])
        part = total([line_ref[k, p] for p in range(depth)])
        part_ref[k, 1] = part
        gath_ref[k, my_plane] = part
        send_all(plane_offsets, plane_peer, lambda peer: part_ref.at[k, 1], gath_ref.at[k, my_plane],
                 gath_send.at[k], gath_recv.at[k])

        @pl.when(k < ITERS - 1)
        def _():
            finish(k + 1, s_ref, sp_ref)
            stack(s_ref[...], sst_ref)

        wait_bytes(gath_ref.at[k], plane - 1, gath_recv.at[k])
        tiles = []
        for t in range(cases // 8):
            tiles.append([])
            for h in range(2):
                at = h * cases + t * 8
                pieces = [
                    gath_ref[k, row // chunk, row % chunk : row % chunk + min(chunk, 8)]
                    for row in range(at, at + 8, min(chunk, 8))
                ]
                tiles[t].append(jnp.concatenate(pieces, axis=0))
        tiles = eliminate(tiles, cases, 4)
        solved_left = jnp.concatenate([tile[0] for tile in tiles], axis=0)
        solved_right = jnp.concatenate([tile[1] for tile in tiles], axis=0)
        step_size = solved_left[:, cases:]
        update = lax.dot_general(solved_right[:, :cases], step_size, NN, precision=HIGH,
                                 preferred_element_type=F32) - solved_right[:, cases:]
        high, low = split2(jnp.concatenate([step_size, update], axis=1))
        cst_ref[...] = jnp.concatenate([high, low, high, low], axis=0)
        mixed_dir = dot(cst_ref[...], dst_ref[...], TN)
        mixed_img = dot(cst_ref[...], ist_ref[...], TN)
        sol_ref[0] = sol_ref[0] + mixed_dir[:cases]
        res_ref[0] = res_ref[0] - mixed_img[:cases]

        @pl.when(k < ITERS - 1)
        def _():
            lin_ref[...] = lin_ref[...] - dot(cst_ref[:, :cases], sst_ref[...], TN)
            dir_ref[...] = weighting * res_ref[0] + mixed_dir[cases:]
            img_ref[...] = lin_ref[...] + mixed_img[cases:]

        wait_bytes(scat_ref.at[k], plane - 1, scat_send.at[k])
        wait_bytes(line_ref.at[k], depth - 1, line_send.at[k])
        wait_bytes(gath_ref.at[k], plane - 1, gath_send.at[k])
        return carry

    lax.fori_loop(0, ITERS, iteration, 0)


def local(cfg, right_side, weights, signs, face_map, pattern, factor):
    cases, unknowns = right_side.shape[1:]
    face = unknowns // 4
    rows_y, z_lo, z_hi, cols_j, chunk = cfg
    plane, depth = rows_y * cols_j, z_lo * z_hi
    field = pltpu.VMEM((cases, unknowns), F32)
    row = pltpu.VMEM((1, unknowns), F32)
    square = pltpu.VMEM((unknowns, unknowns), BF16)
    dma = pltpu.SemaphoreType.DMA
    results = pl.pallas_call(
        functools.partial(kernel, cfg),
        out_shape=(pltpu.VMEM(right_side.shape, F32),) * 2,
        in_specs=[pl.BlockSpec(memory_space=pl.ANY)] + [pl.BlockSpec(memory_space=pltpu.VMEM)] * 3
        + [pl.BlockSpec(memory_space=pltpu.SMEM), pl.BlockSpec(memory_space=pl.ANY)],
        out_specs=(pl.BlockSpec(memory_space=pltpu.VMEM),) * 2,
        scratch_shapes=[
            pltpu.VMEM((1, cases, unknowns), F32), pltpu.VMEM((unknowns, unknowns), F32), square, square, square,
            field, field, field, field, field, field, field,
            pltpu.VMEM((4 * cases, unknowns), BF16), pltpu.VMEM((4 * cases, unknowns), BF16),
            pltpu.VMEM((4 * cases, unknowns), BF16), pltpu.VMEM((4 * cases, 2 * cases), BF16),
            field, field, row, row, row,
            pltpu.VMEM((4, cases + 8, face), F32), pltpu.VMEM((4, cases + 8, face), F32),
            pltpu.VMEM((ITERS, 4, cases, face), F32), pltpu.VMEM((ITERS, 4, cases, face), F32),
            pltpu.VMEM((ITERS, plane, chunk, 128), F32), pltpu.VMEM((ITERS, plane, chunk, 128), F32),
            pltpu.VMEM((ITERS, 2, chunk, 128), F32), pltpu.VMEM((ITERS, depth, chunk, 128), F32),
            pltpu.VMEM((ITERS, plane, chunk, 128), F32),
            dma, dma, dma((4,)), dma((4,)), dma((ITERS, 4)), dma((ITERS, 4)),
            dma((ITERS,)), dma((ITERS,)), dma((ITERS,)), dma((ITERS,)), dma((ITERS,)), dma((ITERS,)),
        ],
        compiler_params=pltpu.CompilerParams(
            collective_id=0, has_side_effects=True, vmem_limit_bytes=60 * 1024 * 1024
        ),
    )(right_side, weights, signs, face_map, pattern, factor)
    return results


def solution(mesh):
    size_x, size_y = mesh.shape["gx"], mesh.shape["gy"]
    z_lo = min(Z_PARTS, size_x // 2)
    z_hi = min(Z_PARTS, size_y // 2)
    rows_y, cols_j = size_x // z_lo, size_y // z_hi
    chunk = 128 // (rows_y * cols_j)
    return jax.shard_map(
        functools.partial(local, (rows_y, z_lo, z_hi, cols_j, chunk)),
        mesh=mesh,
        in_specs=(
            P("gx", None, "gy"),
            P("gx", "gy"),
            P("gx", "gy"),
            P("gx", "gy"),
            P("gx", None, "gy"),
            P("gx", None, "gy"),
        ),
        out_specs=(P("gx", None, "gy"), P("gx", None, "gy")),
        check_vma=False,
    )
```
